32 devices in a mesh: space: 8 (over z, y), chan: 2 (over core), filt: 2 (over x).
Axes of the slice: x: 2, y: 2, z: 4, core: 2. Of those that a mesh axis runs over, the one named last changes fastest.
Arguments:
- activation: bfloat16 [8, 512, 512], P('space', ('chan', 'filt')), may hold values from -6 to 6
- kernel: bfloat16 [3, 3, 3, 512, 512], P(None, None, None, 'filt', 'chan'), may hold values from -0.0546875 to 0.0546875
- out_grad: bfloat16 [8, 512, 512], P('space', 'filt', 'chan'), may hold values from -6 to 6
Outputs:
- output: bfloat16 [8, 512, 512], P('space', 'filt', 'chan')
- input_grad: bfloat16 [8, 512, 512], P('space', ('chan', 'filt'))
- kernel_grad: float32 [3, 3, 3, 512, 512], P(None, None, None, 'filt', 'chan')
The draws below stay inside these ranges and needn't reach their ends.
All inputs are finite; a program needn't handle non-finite values.
Results may differ from the reference program's by a relative error of at most 0.001.
Values may be sent and summed in bfloat16 or wider, within the bound.
A program may use at most 128 MiB of HBM per device.

```python
import jax
import jax.numpy as jnp
from jax import lax

C = 512
F = 512
H = 32
W = 16
NZ = 8


def shard_levels(own_key, shape, split, least, high):
    loudness = 1.0
    for dim, parts in split:
        draws = jax.random.uniform(jax.random.fold_in(jax.random.fold_in(own_key, 6), dim), (parts,), jnp.float32, least / len(split), high / len(split))
        loudness = loudness * jnp.repeat(jnp.exp(draws), shape[dim] // parts).reshape((-1,) + (1,) * (len(shape) - 1 - dim))
    return loudness


def centred(own_key, dims, deviation, bound, cuts=(), kind=jnp.bfloat16):
    level = shard_levels(own_key, dims, cuts, -0.22, 0.18) if cuts else 1.0
    values = jax.random.normal(own_key, dims, jnp.float32) * deviation * level
    return jnp.minimum(jnp.maximum(values, -bound), bound).astype(kind)


def setup_inputs(seed: int = 0) -> dict:
    streams_of = jax.random.split(jax.random.key(seed), 4)
    return {
        "activation": centred(streams_of[0], (NZ, C, H * W), 1.0, 6.0, ((0, 8), (1, 4))),
        "kernel": centred(streams_of[1], (3, 3, 3, F, C), (27 * C) ** -0.5, 0.0546875, ((3, 2), (4, 2))),
        "out_grad": centred(streams_of[2], (NZ, F, H * W), 1.0, 6.0, ((0, 8), (1, 2), (2, 2))),
    }


def reference(activation, kernel, out_grad):
    volume = activation.reshape(NZ, C, H, W).transpose(1, 0, 2, 3)[None]
    result = lax.conv_general_dilated(volume, kernel, (1, 1, 1), 'SAME', dimension_numbers=('NCDHW', 'DHWOI', 'NCDHW'), preferred_element_type=jnp.float32)[0]
    output = result.transpose(1, 0, 2, 3).reshape(NZ, F, H * W).astype(jnp.bfloat16)
    grad_volume = out_grad.reshape(NZ, F, H, W).transpose(1, 0, 2, 3)[None]
    flipped = kernel[::-1, ::-1, ::-1]
    back = lax.conv_general_dilated(grad_volume, flipped, (1, 1, 1), 'SAME', dimension_numbers=('NCDHW', 'DHWIO', 'NCDHW'), preferred_element_type=jnp.float32)[0]
    input_grad = back.transpose(1, 0, 2, 3).reshape(NZ, C, H * W).astype(jnp.bfloat16)
    padded = jnp.pad(activation.reshape(NZ, C, H, W), ((1, 1), (0, 0), (1, 1), (1, 1))).astype(jnp.float32)
    grad_wide = out_grad.astype(jnp.float32)
    taps = []
    for a in range(3):
        for b in range(3):
            for c in range(3):
                piece = padded[a:a + NZ, :, b:b + H, c:c + W].reshape(NZ, C, H * W)
                taps.append(jnp.einsum('zfp,zkp->fk', grad_wide, piece))
    kernel_grad = jnp.stack(taps).reshape(3, 3, 3, F, C) / jnp.sqrt(jnp.float32(NZ * H * W))
    return (output, input_grad, kernel_grad)
```

```python
import functools
import math

import jax
import jax.numpy as jnp
from jax import lax
from jax.experimental import pallas as pl
from jax.experimental.pallas import tpu as pltpu
from jax.sharding import PartitionSpec as P

W = 16
MESH = pl.DeviceIdType.MESH


def shifted_copies(t, store):
    cells = t.shape[0]
    column = lax.broadcasted_iota(jnp.int32, t.shape, 0) % W
    store(0, jnp.where(column >= 1, pltpu.roll(t, 1, 0), 0.0).astype(jnp.bfloat16))
    store(1, t.astype(jnp.bfloat16))
    store(2, jnp.where(column <= W - 2, pltpu.roll(t, cells - 1, 0), 0.0).astype(jnp.bfloat16))


def kernel(
    sizes, act_ref, w_hbm, grad_ref, out_ref, ig_ref, kg_hbm,
    actg, gradg, wide, gwide, w, facc, bacc, fpart, bpart, frecv, brecv, stage,
    w_sem, kg_sem, az_send, ay_send, ax_send, gz_send, gy_send, gc_send,
    a_recv, g_recv, f_send, f_recv, b_send, b_recv,
):
    S, NX, NZ, NY = sizes
    cb, cells = act_ref.shape[1:]
    filters, half = grad_ref.shape[1:]
    chans = NX * cb
    s = lax.axis_index("space")
    c = lax.axis_index("chan")
    x = lax.axis_index("filt")
    z, y = s // NY, s % NY
    oy = (y + 1) % NY
    f32 = jnp.float32

    def remote(src, dst, send, recv, device):
        return pltpu.make_async_remote_copy(
            src_ref=src, dst_ref=dst, send_sem=send, recv_sem=recv,
            device_id=device, device_id_type=MESH,
        )

    zpeers = [{"space": ((z + d) % NZ) * NY + y} for d in range(1, NZ)]
    ypeer = {"space": z * NY + oy}
    xpeers = [{"filt": (x + d) % NX} for d in range(1, NX)]
    cpeer = {"chan": 1 - c}
    barrier = pltpu.get_barrier_semaphore()
    for peer in zpeers + xpeers + [ypeer, cpeer]:
        pl.semaphore_signal(barrier, inc=1, device_id=peer, device_id_type=MESH)
    pl.semaphore_wait(barrier, len(zpeers) + len(xpeers) + 2)

    def a_slot(plane, part):
        return actg.at[plane, pl.ds(pl.multiple_of(part * cb, cb), cb), :]

    def g_slot(plane, part):
        return gradg.at[plane + 1, :, pl.ds(pl.multiple_of(part * half, half), half)]

    def a_z(d):
        return remote(act_ref.at[0], a_slot(s, x), az_send.at[d - 1], a_recv.at[s * NX + x], zpeers[d - 1])

    def g_z(d):
        return remote(grad_ref.at[0], g_slot(s, c), gz_send.at[d - 1], g_recv.at[s * 2 + c], zpeers[d - 1])

    def a_y(k, plane, src):
        return remote(src, a_slot(plane, x), ay_send.at[k], a_recv.at[plane * NX + x], ypeer)

    def g_y(k, plane, src):
        return remote(src, g_slot(plane, c), gy_send.at[k], g_recv.at[plane * 2 + c], ypeer)

    def a_x(k, e, plane, src):
        return remote(
            src, a_slot(plane, x), ax_send.at[k * (NX - 1) + e - 1], a_recv.at[plane * NX + x], xpeers[e - 1]
        )

    def g_c(k, plane, src):
        return remote(src, g_slot(plane, c), gc_send.at[k], g_recv.at[plane * 2 + c], cpeer)

    def a_wait(plane, part):
        a_z_like = remote(
            act_ref.at[0], a_slot(plane, part), az_send.at[0], a_recv.at[plane * NX + part], ypeer
        )
        a_z_like.wait_recv()

    def g_wait(plane, part):
        remote(
            grad_ref.at[0], g_slot(plane, part), gz_send.at[0], g_recv.at[plane * 2 + part], ypeer
        ).wait_recv()

    def mine(d):
        return ((z + d) % NZ) * NY + y

    def other(d):
        return ((z + d) % NZ) * NY + oy

    for d in range(1, NZ):
        g_z(d).start()
        a_z(d).start()
    g_y(0, s, grad_ref.at[0]).start()
    a_y(0, s, act_ref.at[0]).start()
    for e in range(1, NX):
        a_x(0, e, s, act_ref.at[0]).start()
    g_c(0, s, grad_ref.at[0]).start()
    w_copy = pltpu.make_async_copy(w_hbm, w, w_sem)
    w_copy.start()
    actg[s, pl.ds(pl.multiple_of(x * cb, cb), cb), :] = act_ref[0]
    gradg[s + 1, :, pl.ds(pl.multiple_of(c * half, half), half)] = grad_ref[0]
    for end in (0, S + 1):
        gradg[end] = jnp.zeros((filters, cells), jnp.bfloat16)
        wide[end] = jnp.zeros(wide.shape[1:], jnp.bfloat16)

    @pl.loop(1, S + 1)
    def _(j):
        for k in range(3):
            wide[j, k, 0:W, :] = jnp.zeros((W, chans), jnp.bfloat16)
            wide[j, k, W + cells : 2 * W + cells, :] = jnp.zeros((W, chans), jnp.bfloat16)

    for j in range(3):
        for k in range(3):
            gwide[j, k, 0:W, :] = jnp.zeros((W, filters), jnp.bfloat16)
            gwide[j, k, W + cells : 2 * W + cells, :] = jnp.zeros((W, filters), jnp.bfloat16)

    @pl.loop(1, NZ)
    def _(d):
        plane = mine(d)
        g_wait(plane, c)
        g_y(d, plane, g_slot(plane, c)).start()
        g_c(d, plane, g_slot(plane, c)).start()
        a_wait(plane, x)
        a_y(d, plane, a_slot(plane, x)).start()
        for e in range(1, NX):
            a_x(d, e, plane, a_slot(plane, x)).start()

    @pl.loop(0, NZ)
    def _(d):
        plane = other(d)
        a_wait(plane, x)
        for e in range(1, NX):
            a_x(NZ + d, e, plane, a_slot(plane, x)).start()
        g_wait(plane, c)
        g_c(NZ + d, plane, g_slot(plane, c)).start()

    @pl.loop(0, S)
    def _(i):
        plane = (s + i) % S
        g_wait(plane, 1 - c)
        for e in range(1, NX):
            a_wait(plane, (x + e) % NX)

    @pl.loop(0, S)
    def _(i):
        def store(k, value):
            wide[i + 1, k, W : W + cells, :] = value

        shifted_copies(actg[i].astype(f32).T, store)

    @pl.loop(0, 3)
    def _(j):
        def store(k, value):
            gwide[j, k, W : W + cells, :] = value

        shifted_copies(gradg[s + j].astype(f32).T, store)

    w_copy.wait()
    facc[...] = jnp.zeros_like(facc)
    bacc[...] = jnp.zeros_like(bacc)

    @pl.loop(0, 9)
    def _(i):
        a, b = i // 3, i % 3
        total = None
        for k in range(3):
            rows = wide[s + a, k, pl.ds(pl.multiple_of(b * W, W), cells), :]
            term = lax.dot_general(rows, w[a, b, k], (((1,), (1,)), ((), ())), preferred_element_type=f32)
            total = term if total is None else total + term
        facc[...] += total

    fpart[...] = facc[...].T
    f_copy = remote(
        fpart.at[:, pl.ds(pl.multiple_of((1 - c) * half, half), half)], frecv, f_send, f_recv, cpeer
    )
    f_copy.start()

    @pl.loop(0, 9)
    def _(i):
        a, b = i // 3, i % 3
        total = None
        for k in range(3):
            rows = gwide[2 - a, 2 - k, pl.ds(pl.multiple_of((2 - b) * W, W), cells), :]
            term = jnp.dot(rows, w[a, b, k], preferred_element_type=f32)
            total = term if total is None else total + term
        bacc[...] += total

    bpart[...] = bacc[...].T

    def b_copy(e):
        to = (x + e) % NX
        return remote(
            bpart.at[pl.ds(pl.multiple_of(to * cb, cb), cb), :],
            brecv.at[e - 1], b_send.at[e - 1], b_recv.at[e - 1], xpeers[e - 1],
        )

    for e in range(1, NX):
        b_copy(e).start()

    scale = 1.0 / math.sqrt(S * cells)
    group = 4

    def kg_copy(i, j):
        return pltpu.make_async_copy(stage.at[i, j], kg_hbm.at[2 - j, i // 3, i % 3], kg_sem.at[i * 3 + j])

    @pl.loop(0, 9)
    def _(i):
        b, k = i // 3, i % 3

        @pl.loop(0, S // group)
        def _(q):
            total = None
            for n in range(group):
                j = q * group + n
                rows = wide[j + 1, k, pl.ds(pl.multiple_of(b * W, W), cells), :]
                grads = gradg[pl.ds(j, 3)].reshape(3 * filters, cells)
                term = jnp.dot(grads, rows, preferred_element_type=f32)
                total = term if total is None else total + term
            total = (total * scale).reshape(3, filters, chans)

            @pl.when(q == 0)
            def _():
                stage[i] = total

            @pl.when(q > 0)
            def _():
                stage[i] += total

        for j in range(3):
            kg_copy(i, j).start()

    f_copy.wait()
    out_ref[0] = (fpart[:, pl.ds(pl.multiple_of(c * half, half), half)] + frecv[...]).astype(jnp.bfloat16)
    own = bpart[pl.ds(pl.multiple_of(x * cb, cb), cb), :]
    for e in range(1, NX):
        b_copy(e).wait()
        own = own + brecv[e - 1]
    ig_ref[0] = own.astype(jnp.bfloat16)

    for d in range(1, NZ):
        a_z(d).wait_send()
        g_z(d).wait_send()

    @pl.loop(0, NZ)
    def _(d):
        a_y(d, mine(d), a_slot(mine(d), x)).wait_send()
        g_y(d, mine(d), g_slot(mine(d), c)).wait_send()

    @pl.loop(0, S)
    def _(k):
        for e in range(1, NX):
            a_x(k, e, s, a_slot(s, x)).wait_send()
        g_c(k, s, g_slot(s, c)).wait_send()

    @pl.loop(0, 9)
    def _(i):
        for j in range(3):
            kg_copy(i, j).wait()


def body(activation, weights, out_grad):
    S = lax.axis_size("space")
    NX = lax.axis_size("filt")
    NY = 2
    NZ = S // NY
    cb, cells = activation.shape[1:]
    filters, half = out_grad.shape[1:]
    chans = NX * cb
    bf16, f32 = jnp.bfloat16, jnp.float32
    dma = pltpu.SemaphoreType.DMA
    vmem = pl.BlockSpec(memory_space=pltpu.VMEM)
    hbm = pl.BlockSpec(memory_space=pl.ANY)
    return pl.pallas_call(
        functools.partial(kernel, (S, NX, NZ, NY)),
        out_shape=(
            jax.ShapeDtypeStruct(out_grad.shape, bf16),
            jax.ShapeDtypeStruct(activation.shape, bf16),
            jax.ShapeDtypeStruct(weights.shape, f32),
        ),
        in_specs=[vmem, hbm, vmem],
        out_specs=(vmem, vmem, hbm),
        scratch_shapes=[
            pltpu.VMEM((S, chans, cells), bf16),
            pltpu.VMEM((S + 2, filters, cells), bf16),
            pltpu.VMEM((S + 2, 3, cells + 2 * W, chans), bf16),
            pltpu.VMEM((3, 3, cells + 2 * W, filters), bf16),
            pltpu.VMEM(weights.shape, bf16),
            pltpu.VMEM((cells, filters), f32),
            pltpu.VMEM((cells, chans), f32),
            pltpu.VMEM((filters, cells), f32),
            pltpu.VMEM((chans, cells), f32),
            pltpu.VMEM((filters, half), f32),
            pltpu.VMEM((NX - 1, cb, cells), f32),
            pltpu.VMEM((9, 3, filters, chans), f32),
            dma, dma((27,)),
            dma((NZ - 1,)), dma((NZ,)), dma((S * (NX - 1),)),
            dma((NZ - 1,)), dma((NZ,)), dma((S,)),
            dma((S * NX,)), dma((S * 2,)),
            dma, dma, dma((NX - 1,)), dma((NX - 1,)),
        ],
        compiler_params=pltpu.CompilerParams(
            collective_id=0, has_side_effects=True, vmem_limit_bytes=56 * 1024 * 1024
        ),
    )(activation, weights, out_grad)


def solution(mesh):
    placed = (
        P("space", ("chan", "filt"), None),
        P(None, None, None, "filt", "chan"),
        P("space", "filt", "chan"),
    )
    return jax.shard_map(
        body,
        mesh=mesh,
        in_specs=placed,
        out_specs=(
            P("space", "filt", "chan"),
            P("space", ("chan", "filt"), None),
            P(None, None, None, "filt", "chan"),
        ),
        check_vma=False,
    )
```

```python
import functools
import math

import jax
import jax.numpy as jnp
from jax import lax
from jax.experimental import pallas as pl
from jax.experimental.pallas import tpu as pltpu
from jax.sharding import PartitionSpec as P

W = 16
MESH = pl.DeviceIdType.MESH


def shifted_copies(t, store):
    cells = t.shape[0]
    column = lax.broadcasted_iota(jnp.int32, t.shape, 0) % W
    store(0, jnp.where(column >= 1, pltpu.roll(t, 1, 0), 0.0).astype(jnp.bfloat16))
    store(1, t.astype(jnp.bfloat16))
    store(2, jnp.where(column <= W - 2, pltpu.roll(t, cells - 1, 0), 0.0).astype(jnp.bfloat16))


def kernel(
    sizes, act_ref, w_hbm, grad_ref, out_ref, ig_ref, acc,
    actg, gradg, wide, gwide, w, facc, bacc, fpart, bpart, frecv, brecv,
    w_sem, az_send, ay_send, ax_send, gz_send, gy_send, gc_send,
    a_recv, g_recv, f_send, f_recv, b_send, b_recv,
):
    S, NX, NZ, NY = sizes
    cb, cells = act_ref.shape[1:]
    filters, half = grad_ref.shape[1:]
    chans = NX * cb
    s = lax.axis_index("space")
    c = lax.axis_index("chan")
    x = lax.axis_index("filt")
    z, y = s // NY, s % NY
    oy = 1 - y
    f32, bf16 = jnp.float32, jnp.bfloat16

    def remote(src, dst, send, recv, device):
        return pltpu.make_async_remote_copy(
            src_ref=src, dst_ref=dst, send_sem=send, recv_sem=recv,
            device_id=device, device_id_type=MESH,
        )

    def signal(device):
        pl.semaphore_signal(barrier, inc=1, device_id=device, device_id_type=MESH)

    def a_slot(plane, part):
        return actg.at[plane, pl.ds(pl.multiple_of(part * cb, cb), cb), :]

    def g_slot(plane, part):
        return gradg.at[plane + 1, :, pl.ds(pl.multiple_of(part * half, half), half)]

    ypeer = {"space": z * NY + oy}
    xpeers = [{"filt": (x + e) % NX} for e in range(1, NX)]
    cpeer = {"chan": 1 - c}

    def a_copy(plane, send, device):
        slot = a_slot(plane, x)
        return remote(slot, slot, send, a_recv.at[plane * NX + x], device)

    def g_copy(plane, send, device):
        slot = g_slot(plane, c)
        return remote(slot, slot, send, g_recv.at[plane * 2 + c], device)

    def a_wait(plane, part):
        slot = a_slot(plane, part)
        remote(slot, slot, ay_send.at[0], a_recv.at[plane * NX + part], ypeer).wait_recv()

    def g_wait(plane, part):
        slot = g_slot(plane, part)
        remote(slot, slot, gy_send.at[0], g_recv.at[plane * 2 + part], ypeer).wait_recv()

    def a_z(zz, way):
        to = {"space": (z + way) * NY + y}
        return a_copy(zz * NY + y, az_send.at[(way + 1) // 2 * NZ + zz], to)

    def g_z(zz, way):
        to = {"space": (z + way) * NY + y}
        return g_copy(zz * NY + y, gz_send.at[(way + 1) // 2 * NZ + zz], to)

    def a_y(zz):
        return a_copy(zz * NY + y, ay_send.at[zz], ypeer)

    def g_y(zz):
        return g_copy(zz * NY + y, gy_send.at[zz], ypeer)

    def a_x(plane, e):
        return a_copy(plane, ax_send.at[plane * (NX - 1) + e - 1], xpeers[e - 1])

    def g_c(plane):
        return g_copy(plane, gc_send.at[plane], cpeer)

    def start_x(plane):
        for e in range(1, NX):
            a_x(plane, e).start()

    def inside(zz):
        return (zz >= 0) & (zz < NZ)

    def at_distance(d, run):
        @pl.when(inside(z - d))
        def _():
            run(z - d, -1)

        @pl.when((d > 0) & inside(z + d))
        def _():
            run(z + d, 1)

    actg[s, pl.ds(pl.multiple_of(x * cb, cb), cb), :] = act_ref[0]
    gradg[s + 1, :, pl.ds(pl.multiple_of(c * half, half), half)] = grad_ref[0]
    barrier = pltpu.get_barrier_semaphore()
    for way in (-1, 1):
        @pl.when(inside(z + way))
        def _():
            signal({"space": (z + way) * NY + y})
    for peer in [ypeer, cpeer] + xpeers:
        signal(peer)
    beside = (z + NZ - 1) // NZ + (2 * NZ - 2 - z) // NZ
    pl.semaphore_wait(barrier, NX + 1 + beside)

    for way in (-1, 1):
        @pl.when(inside(z + way))
        def _():
            a_z(z, way).start()
    a_y(z).start()
    start_x(s)
    for way in (-1, 1):
        @pl.when(inside(z + way))
        def _():
            g_z(z, way).start()
    g_y(z).start()
    g_c(s).start()
    w_copy = pltpu.make_async_copy(w_hbm, w, w_sem)
    w_copy.start()

    for end in (0, S + 1):
        gradg[end] = jnp.zeros((filters, cells), bf16)
        wide[end] = jnp.zeros(wide.shape[1:], bf16)

    @pl.loop(1, S + 1)
    def _(j):
        for k in range(3):
            wide[j, k, 0:W, :] = jnp.zeros((W, chans), bf16)
            wide[j, k, W + cells : 2 * W + cells, :] = jnp.zeros((W, chans), bf16)

    for j in range(3):
        for k in range(3):
            gwide[j, k, 0:W, :] = jnp.zeros((W, filters), bf16)
            gwide[j, k, W + cells : 2 * W + cells, :] = jnp.zeros((W, filters), bf16)

    @pl.loop(0, 27)
    def _(i):
        acc[i // 9, i // 3 % 3, i % 3] = jnp.zeros((filters, chans), f32)

    facc[...] = jnp.zeros_like(facc)
    bacc[...] = jnp.zeros_like(bacc)
    w_copy.wait()

    def b_copy(e):
        to = (x + e) % NX
        return remote(
            bpart.at[pl.ds(pl.multiple_of(to * cb, cb), cb), :],
            brecv.at[e - 1], b_send.at[e - 1], b_recv.at[e - 1], xpeers[e - 1],
        )

    f_copy = remote(
        fpart.at[:, pl.ds(pl.multiple_of((1 - c) * half, half), half)], frecv, f_send, f_recv, cpeer
    )

    def backward():
        @pl.loop(0, 3)
        def _(j):
            def store(k, value):
                gwide[j, k, W : W + cells, :] = value

            shifted_copies(gradg[s + j].astype(f32).T, store)

        @pl.loop(0, 9)
        def _(i):
            a, b = i // 3, i % 3
            total = None
            for k in range(3):
                rows = gwide[2 - a, 2 - k, pl.ds(pl.multiple_of((2 - b) * W, W), cells), :]
                term = jnp.dot(rows, w[a, b, k], preferred_element_type=f32)
                total = term if total is None else total + term
            bacc[...] += total

        bpart[...] = bacc[...].T
        for e in range(1, NX):
            b_copy(e).start()

    def forward():
        @pl.loop(0, 9)
        def _(i):
            a, b = i // 3, i % 3
            total = None
            for k in range(3):
                rows = wide[s + a, k, pl.ds(pl.multiple_of(b * W, W), cells), :]
                term = lax.dot_general(rows, w[a, b, k], (((1,), (1,)), ((), ())), preferred_element_type=f32)
                total = term if total is None else total + term
            facc[...] += total

        fpart[...] = facc[...].T
        f_copy.start()

    def prepare(zz):
        @pl.loop(0, NY)
        def _(i):
            plane = zz * NY + i
            for e in range(1, NX):
                a_wait(plane, (x + e) % NX)

            def store(k, value):
                wide[plane + 1, k, W : W + cells, :] = value

            shifted_copies(actg[plane].astype(f32).T, store)

    scale = 1.0 / math.sqrt(S * cells)

    def filter_grad(zz):
        @pl.loop(0, 9)
        def _(i):
            b, k = i // 3, i % 3
            total = None
            for n in range(NY):
                j = zz * NY + n
                rows = wide[j + 1, k, pl.ds(pl.multiple_of(b * W, W), cells), :]
                grads = gradg[pl.ds(j, 3)].reshape(3 * filters, cells)
                term = jnp.dot(grads, rows, preferred_element_type=f32)
                total = term if total is None else total + term
            for j in range(3):
                acc[2 - j, b, k] += total[j * filters : (j + 1) * filters] * scale

    def relay(zz, way, wait, along, across, last):
        plane = zz * NY + y
        wait(plane)

        @pl.when(inside(z - way))
        def _():
            along(zz, -way).start()

        across(zz).start()
        last(plane)

    def pass_on(zz, wait, last):
        plane = zz * NY + oy
        wait(plane)
        last(plane)

    def a_own(plane):
        a_wait(plane, x)

    def g_own(plane):
        g_wait(plane, c)

    def start_c(plane):
        g_c(plane).start()

    def core_halves(zz, way):
        for n in range(NY):
            g_wait(zz * NY + n, 1 - c)

    @pl.loop(1, NZ + 2)
    def _(d):
        at_distance(d - 1, lambda zz, way: pass_on(zz, a_own, start_x))
        at_distance(d, lambda zz, way: relay(zz, way, a_own, a_z, a_y, start_x))
        at_distance(d - 1, lambda zz, way: pass_on(zz, g_own, start_c))
        at_distance(d, lambda zz, way: relay(zz, way, g_own, g_z, g_y, start_c))
        at_distance(d - 1, core_halves)

        @pl.when(d == 2)
        def _():
            backward()

        @pl.when(d >= 2)
        def _():
            at_distance(d - 2, lambda zz, way: prepare(zz))

        @pl.when(d == 3)
        def _():
            forward()

        @pl.when(d >= 2)
        def _():
            at_distance(d - 2, lambda zz, way: filter_grad(zz))

    f_copy.wait()
    out_ref[0] = (fpart[:, pl.ds(pl.multiple_of(c * half, half), half)] + frecv[...]).astype(bf16)
    own = bpart[pl.ds(pl.multiple_of(x * cb, cb), cb), :]
    for e in range(1, NX):
        b_copy(e).wait()
        own = own + brecv[e - 1]
    ig_ref[0] = own.astype(bf16)

    @pl.loop(0, NZ)
    def _(zz):
        for way in (-1, 1):
            @pl.when(inside(z + way) & ((z - zz) * way >= 0))
            def _():
                a_z(zz, way).wait_send()
                g_z(zz, way).wait_send()
        a_y(zz).wait_send()
        g_y(zz).wait_send()

    @pl.loop(0, S)
    def _(plane):
        for e in range(1, NX):
            a_x(plane, e).wait_send()
        g_c(plane).wait_send()


def body(activation, weights, out_grad):
    S = lax.axis_size("space")
    NX = lax.axis_size("filt")
    NY = 2
    NZ = S // NY
    cb, cells = activation.shape[1:]
    filters, half = out_grad.shape[1:]
    chans = NX * cb
    bf16, f32 = jnp.bfloat16, jnp.float32
    dma = pltpu.SemaphoreType.DMA
    vmem = pl.BlockSpec(memory_space=pltpu.VMEM)
    hbm = pl.BlockSpec(memory_space=pl.ANY)
    shapes = ((out_grad.shape, bf16), (activation.shape, bf16), (weights.shape, f32))
    results = pl.pallas_call(
        functools.partial(kernel, (S, NX, NZ, NY)),
        out_shape=tuple(pltpu.VMEM(*shape) for shape in shapes),
        in_specs=[vmem, hbm, vmem],
        out_specs=(vmem, vmem, vmem),
        scratch_shapes=[
            pltpu.VMEM((S, chans, cells), bf16),
            pltpu.VMEM((S + 2, filters, cells), bf16),
            pltpu.VMEM((S + 2, 3, cells + 2 * W, chans), bf16),
            pltpu.VMEM((3, 3, cells + 2 * W, filters), bf16),
            pltpu.VMEM(weights.shape, bf16),
            pltpu.VMEM((cells, filters), f32),
            pltpu.VMEM((cells, chans), f32),
            pltpu.VMEM((filters, cells), f32),
            pltpu.VMEM((chans, cells), f32),
            pltpu.VMEM((filters, half), f32),
            pltpu.VMEM((NX - 1, cb, cells), f32),
            dma,
            dma((2 * NZ,)), dma((NZ,)), dma((S * (NX - 1),)),
            dma((2 * NZ,)), dma((NZ,)), dma((S,)),
            dma((S * NX,)), dma((S * 2,)),
            dma, dma, dma((NX - 1,)), dma((NX - 1,)),
        ],
        compiler_params=pltpu.CompilerParams(
            collective_id=0, has_side_effects=True, vmem_limit_bytes=50 * 1024 * 1024
        ),
    )(activation, weights, out_grad)
    return results


def solution(mesh):
    placed = (
        P("space", ("chan", "filt"), None),
        P(None, None, None, "filt", "chan"),
        P("space", "filt", "chan"),
    )
    return jax.shard_map(
        body,
        mesh=mesh,
        in_specs=placed,
        out_specs=(
            P("space", "filt", "chan"),
            P("space", ("chan", "filt"), None),
            P(None, None, None, "filt", "chan"),
        ),
        check_vma=False,
    )
```

```python
import functools
import math

import jax
import jax.numpy as jnp
from jax import lax
from jax.experimental import pallas as pl
from jax.experimental.pallas import tpu as pltpu
from jax.sharding import PartitionSpec as P

W = 16
MESH = pl.DeviceIdType.MESH


def shifted_copies(t, store):
    cells = t.shape[0]
    column = lax.broadcasted_iota(jnp.int32, t.shape, 0) % W
    store(0, jnp.where(column >= 1, pltpu.roll(t, 1, 0), 0.0).astype(jnp.bfloat16))
    store(1, t.astype(jnp.bfloat16))
    store(2, jnp.where(column <= W - 2, pltpu.roll(t, cells - 1, 0), 0.0).astype(jnp.bfloat16))


def kernel(
    sizes, act_ref, w_hbm, grad_ref, out_ref, ig_ref, acc,
    actg, gradg, wide, gwide, w, wf, facc, bacc, fpart, bpart, frecv, brecv,
    w_sem, wf_sem, az_send, ay_send, ax_send, gz_send, gy_send, gc_send,
    a_recv, g_recv, f_send, f_recv, b_send, b_recv,
):
    S, NX, NZ, NY = sizes
    cb, cells = act_ref.shape[1:]
    filters, half = grad_ref.shape[1:]
    chans = NX * cb
    s = lax.axis_index("space")
    c = lax.axis_index("chan")
    x = lax.axis_index("filt")
    z, y = s // NY, s % NY
    oy = 1 - y
    f32, bf16 = jnp.float32, jnp.bfloat16

    def remote(src, dst, send, recv, device):
        return pltpu.make_async_remote_copy(
            src_ref=src, dst_ref=dst, send_sem=send, recv_sem=recv,
            device_id=device, device_id_type=MESH,
        )

    def signal(device):
        pl.semaphore_signal(barrier, inc=1, device_id=device, device_id_type=MESH)

    def a_slot(plane, part):
        return actg.at[plane, pl.ds(pl.multiple_of(part * cb, cb), cb), :]

    def g_slot(plane, part):
        return gradg.at[plane + 1, :, pl.ds(pl.multiple_of(part * half, half), half)]

    ypeer = {"space": z * NY + oy}
    xpeers = [{"filt": (x + e) % NX} for e in range(1, NX)]
    cpeer = {"chan": 1 - c}

    def a_copy(plane, send, device):
        slot = a_slot(plane, x)
        return remote(slot, slot, send, a_recv.at[plane * NX + x], device)

    def g_copy(plane, send, device):
        slot = g_slot(plane, c)
        return remote(slot, slot, send, g_recv.at[plane * 2 + c], device)

    def a_wait(plane, part):
        slot = a_slot(plane, part)
        remote(slot, slot, ay_send.at[0], a_recv.at[plane * NX + part], ypeer).wait_recv()

    def g_wait(plane, part):
        slot = g_slot(plane, part)
        remote(slot, slot, gy_send.at[0], g_recv.at[plane * 2 + part], ypeer).wait_recv()

    def a_z(zz, way):
        to = {"space": (z + way) * NY + y}
        return a_copy(zz * NY + y, az_send.at[(way + 1) // 2 * NZ + zz], to)

    def g_z(zz, way):
        to = {"space": (z + way) * NY + y}
        return g_copy(zz * NY + y, gz_send.at[(way + 1) // 2 * NZ + zz], to)

    def a_y(zz):
        return a_copy(zz * NY + y, ay_send.at[zz], ypeer)

    def g_y(zz):
        return g_copy(zz * NY + y, gy_send.at[zz], ypeer)

    def a_x(plane, e):
        return a_copy(plane, ax_send.at[plane * (NX - 1) + e - 1], xpeers[e - 1])

    def g_c(plane):
        return g_copy(plane, gc_send.at[plane], cpeer)

    def start_x(plane):
        for e in range(1, NX):
            a_x(plane, e).start()

    def inside(zz):
        return (zz >= 0) & (zz < NZ)

    def at_distance(d, run):
        @pl.when(inside(z - d))
        def _():
            run(z - d, -1)

        @pl.when((d > 0) & inside(z + d))
        def _():
            run(z + d, 1)

    actg[s, pl.ds(pl.multiple_of(x * cb, cb), cb), :] = act_ref[0]
    gradg[s + 1, :, pl.ds(pl.multiple_of(c * half, half), half)] = grad_ref[0]
    barrier = pltpu.get_barrier_semaphore()
    for way in (-1, 1):
        @pl.when(inside(z + way))
        def _():
            signal({"space": (z + way) * NY + y})
    for peer in [ypeer, cpeer] + xpeers:
        signal(peer)
    beside = (z + NZ - 1) // NZ + (2 * NZ - 2 - z) // NZ
    pl.semaphore_wait(barrier, NX + 1 + beside)

    for way in (-1, 1):
        @pl.when(inside(z + way))
        def _():
            a_z(z, way).start()
    a_y(z).start()
    start_x(s)
    for way in (-1, 1):
        @pl.when(inside(z + way))
        def _():
            g_z(z, way).start()
    g_y(z).start()
    g_c(s).start()
    w_copy = pltpu.make_async_copy(w_hbm, w, w_sem)
    w_copy.start()

    def wf_copy(i):
        a, b, k = i // 9, i // 3 % 3, i % 3
        return pltpu.make_async_copy(
            w_hbm.at[a, b, k], wf.at[a, b, :, k * chans : (k + 1) * chans], wf_sem.at[i]
        )

    for i in range(27):
        wf_copy(i).start()

    for end in (0, S + 1):
        gradg[end] = jnp.zeros((filters, cells), bf16)
        wide[end] = jnp.zeros(wide.shape[1:], bf16)

    @pl.loop(1, S + 1)
    def _(j):
        wide[j, 0:W, :] = jnp.zeros((W, 3 * chans), bf16)
        wide[j, W + cells : 2 * W + cells, :] = jnp.zeros((W, 3 * chans), bf16)

    for j in range(3):
        gwide[j, 0:W, :] = jnp.zeros((W, gwide.shape[2]), bf16)
        gwide[j, W + cells : 2 * W + cells, :] = jnp.zeros((W, gwide.shape[2]), bf16)

    @pl.loop(0, 27)
    def _(i):
        acc[i // 9, i // 3 % 3, i % 3] = jnp.zeros((filters, chans), f32)

    facc[...] = jnp.zeros_like(facc)
    bacc[...] = jnp.zeros_like(bacc)
    w_copy.wait()
    for i in range(27):
        wf_copy(i).wait()

    lanes = gwide.shape[2] // 3

    def b_copy(e):
        to = (x + e) % NX
        return remote(
            bpart.at[pl.ds(pl.multiple_of(to * cb, cb), cb), :],
            brecv.at[e - 1], b_send.at[e - 1], b_recv.at[e - 1], xpeers[e - 1],
        )

    f_copy = remote(
        fpart.at[:, pl.ds(pl.multiple_of((1 - c) * half, half), half)], frecv, f_send, f_recv, cpeer
    )

    def window(plane, b):
        return wide[plane + 1, pl.ds(pl.multiple_of(b * W, W), cells), :]

    def backward():
        @pl.loop(0, 3)
        def _(j):
            def store(k, value):
                at = (2 - k) * lanes
                gwide[j, W : W + cells, at : at + filters] = value

            shifted_copies(gradg[s + j].astype(f32).T, store)

        @pl.loop(0, 3)
        def _(a):
            total = None
            for b in range(3):
                rows = slice((2 - b) * W, (2 - b) * W + cells)
                if lanes == filters:
                    taps = w[a, b].reshape(3 * filters, chans)
                    terms = [jnp.dot(gwide[2 - a, rows, :], taps, preferred_element_type=f32)]
                else:
                    terms = [
                        jnp.dot(
                            gwide[2 - a, rows, k * lanes : k * lanes + filters],
                            w[a, b, k], preferred_element_type=f32,
                        )
                        for k in range(3)
                    ]
                for term in terms:
                    total = term if total is None else total + term
            bacc[...] += total

        bpart[...] = bacc[...].T

    def send_backward():
        for e in range(1, NX):
            b_copy(e).start()

    def forward():
        @pl.loop(0, 3)
        def _(a):
            total = None
            for b in range(3):
                term = lax.dot_general(
                    window(s + a - 1, b), wf[a, b], (((1,), (1,)), ((), ())), preferred_element_type=f32
                )
                total = term if total is None else total + term
            facc[...] += total

        fpart[...] = facc[...].T
        f_copy.start()

    def prepare(zz):
        @pl.loop(0, NY)
        def _(i):
            plane = zz * NY + i
            for e in range(1, NX):
                a_wait(plane, (x + e) % NX)

            def store(k, value):
                wide[plane + 1, W : W + cells, k * chans : (k + 1) * chans] = value

            shifted_copies(actg[plane].astype(f32).T, store)

    scale = 1.0 / math.sqrt(S * cells)

    def add(a, b, value):
        for k in range(3):
            acc[a, b, k] += value[:, k * chans : (k + 1) * chans] * scale

    def in_pair(zz):
        @pl.loop(0, 3)
        def _(b):
            j = zz * NY
            grads = gradg[pl.ds(j + 1, 2)].reshape(2 * filters, cells)
            low = jnp.dot(grads, window(j, b), preferred_element_type=f32)
            high = jnp.dot(grads, window(j + 1, b), preferred_element_type=f32)
            add(0, b, low[filters:])
            add(1, b, low[:filters] + high[filters:])
            add(2, b, high[:filters])

    def across_pairs(zz):
        @pl.loop(0, 3)
        def _(b):
            j = zz * NY + 1
            add(0, b, jnp.dot(gradg[j + 2], window(j, b), preferred_element_type=f32))
            add(2, b, jnp.dot(gradg[j + 1], window(j + 1, b), preferred_element_type=f32))

    def filter_grad(zz, way):
        prepare(zz)
        in_pair(zz)

        @pl.when(zz != z)
        def _():
            across_pairs(zz + (-1 - way) // 2)

    def relay(zz, way, wait, along, across, last):
        plane = zz * NY + y
        wait(plane)

        @pl.when(inside(z - way))
        def _():
            along(zz, -way).start()

        across(zz).start()
        last(plane)

    def pass_on(zz, wait, last):
        plane = zz * NY + oy
        wait(plane)
        last(plane)

    def a_own(plane):
        a_wait(plane, x)

    def g_own(plane):
        g_wait(plane, c)

    def start_c(plane):
        g_c(plane).start()

    def core_halves(zz, way):
        for n in range(NY):
            g_wait(zz * NY + n, 1 - c)

    @pl.loop(1, NZ + 2)
    def _(d):
        at_distance(d - 1, lambda zz, way: pass_on(zz, a_own, start_x))
        at_distance(d, lambda zz, way: relay(zz, way, a_own, a_z, a_y, start_x))
        at_distance(d - 1, lambda zz, way: pass_on(zz, g_own, start_c))
        at_distance(d, lambda zz, way: relay(zz, way, g_own, g_z, g_y, start_c))
        at_distance(d - 1, core_halves)

        @pl.when(d == 2)
        def _():
            backward()

        @pl.when(d == 4)
        def _():
            send_backward()
            forward()

        @pl.when(d != 2)
        def _():
            at_distance(jnp.maximum(d - 2, 0), filter_grad)

    f_copy.wait()
    out_ref[0] = (fpart[:, pl.ds(pl.multiple_of(c * half, half), half)] + frecv[...]).astype(bf16)
    own = bpart[pl.ds(pl.multiple_of(x * cb, cb), cb), :]
    for e in range(1, NX):
        b_copy(e).wait()
        own = own + brecv[e - 1]
    ig_ref[0] = own.astype(bf16)

    @pl.loop(0, NZ)
    def _(zz):
        for way in (-1, 1):
            @pl.when(inside(z + way) & ((z - zz) * way >= 0))
            def _():
                a_z(zz, way).wait_send()
                g_z(zz, way).wait_send()
        a_y(zz).wait_send()
        g_y(zz).wait_send()

    @pl.loop(0, S)
    def _(plane):
        for e in range(1, NX):
            a_x(plane, e).wait_send()
        g_c(plane).wait_send()


def body(activation, weights, out_grad):
    S = lax.axis_size("space")
    NX = lax.axis_size("filt")
    NY = 2
    NZ = S // NY
    cb, cells = activation.shape[1:]
    filters, half = out_grad.shape[1:]
    chans = NX * cb
    bf16, f32 = jnp.bfloat16, jnp.float32
    dma = pltpu.SemaphoreType.DMA
    vmem = pl.BlockSpec(memory_space=pltpu.VMEM)
    hbm = pl.BlockSpec(memory_space=pl.ANY)
    shapes = ((out_grad.shape, bf16), (activation.shape, bf16), (weights.shape, f32))
    results = pl.pallas_call(
        functools.partial(kernel, (S, NX, NZ, NY)),
        out_shape=tuple(pltpu.VMEM(*shape) for shape in shapes),
        in_specs=[vmem, hbm, vmem],
        out_specs=(vmem, vmem, vmem),
        scratch_shapes=[
            pltpu.VMEM((S, chans, cells), bf16),
            pltpu.VMEM((S + 2, filters, cells), bf16),
            pltpu.VMEM((S + 2, cells + 2 * W, 3 * chans), bf16),
            pltpu.VMEM((3, cells + 2 * W, 3 * pl.cdiv(filters, 128) * 128), bf16),
            pltpu.VMEM(weights.shape, bf16),
            pltpu.VMEM((3, 3, filters, 3 * chans), bf16),
            pltpu.VMEM((cells, filters), f32),
            pltpu.VMEM((cells, chans), f32),
            pltpu.VMEM((filters, cells), f32),
            pltpu.VMEM((chans, cells), f32),
            pltpu.VMEM((filters, half), f32),
            pltpu.VMEM((NX - 1, cb, cells), f32),
            dma, dma((27,)),
            dma((2 * NZ,)), dma((NZ,)), dma((S * (NX - 1),)),
            dma((2 * NZ,)), dma((NZ,)), dma((S,)),
            dma((S * NX,)), dma((S * 2,)),
            dma, dma, dma((NX - 1,)), dma((NX - 1,)),
        ],
        compiler_params=pltpu.CompilerParams(
            collective_id=0, has_side_effects=True, vmem_limit_bytes=50 * 1024 * 1024
        ),
    )(activation, weights, out_grad)
    return results


def solution(mesh):
    placed = (
        P("space", ("chan", "filt"), None),
        P(None, None, None, "filt", "chan"),
        P("space", "filt", "chan"),
    )
    return jax.shard_map(
        body,
        mesh=mesh,
        in_specs=placed,
        out_specs=(
            P("space", "filt", "chan"),
            P("space", ("chan", "filt"), None),
            P(None, None, None, "filt", "chan"),
        ),
        check_vma=False,
    )
```
